32 devices in a mesh: dp: 4 (over y, x), seq: 4 (over z), tensor: 2 (over core).
Axes of the slice: x: 2, y: 2, z: 4, core: 2. Of those that a mesh axis runs over, the one named last changes fastest.
Arguments:
- hidden: bfloat16 [8, 1024, 768], P('dp', 'seq'), may hold values from -6 to 6
- cotangent: bfloat16 [8, 1024, 768], P('dp', 'seq'), may hold values from -6 to 6
- gating: float32 [768, 1536], P(('dp', 'seq'), 'tensor'), may hold values from -0.21875 to 0.21875
- values: float32 [768, 1536], P(('dp', 'seq'), 'tensor'), may hold values from -0.21875 to 0.21875
- selector: float32 [768, 256], P(('dp', 'seq'), 'tensor'), may hold values from -0.21875 to 0.21875
- timestep: float32 [768, 24], P(('dp', 'seq'), 'tensor'), may hold values from -0.4375 to 0.4375
- output: float32 [1536, 768], P('tensor', ('dp', 'seq')), may hold values from -0.15625 to 0.15625
- prenorm: float32 [768], P(('dp', 'seq')), may hold values from 0.5 to 1.5
- postnorm: float32 [1536], P('tensor'), may hold values from 0.5 to 1.5
- filters: float32 [5, 1536], P(None, 'tensor'), may hold values from -3 to 3
- kernels: float32 [5, 256], P(None, 'tensor'), may hold values from -3 to 3
- scalars: float32 [3, 24], P(None, 'tensor'), may hold values from -14 to 2
- gating_adam: float32 [2, 768, 1536], P(None, ('dp', 'seq'), 'tensor'), may hold values from -2 to 2, as said below
- values_adam: float32 [2, 768, 1536], P(None, ('dp', 'seq'), 'tensor'), may hold values from -2 to 2, as said below
- selector_adam: float32 [2, 768, 256], P(None, ('dp', 'seq'), 'tensor'), may hold values from -2 to 2, as said below
- timestep_adam: float32 [2, 768, 24], P(None, ('dp', 'seq'), 'tensor'), may hold values from -2 to 2, as said below
- output_adam: float32 [2, 1536, 768], P(None, 'tensor', ('dp', 'seq')), may hold values from -2 to 2, as said below
- prenorm_adam: float32 [2, 768], P(None, ('dp', 'seq')), may hold values from -97 to 97, as said below
- postnorm_adam: float32 [2, 1536], P(None, 'tensor'), may hold values from -2 to 2, as said below
- filters_adam: float32 [2, 5, 1536], P(None, None, 'tensor'), may hold values from -2 to 2, as said below
- kernels_adam: float32 [2, 5, 256], P(None, None, 'tensor'), may hold values from -2 to 2, as said below
- scalars_adam: float32 [2, 3, 24], P(None, None, 'tensor'), may hold values from -2 to 2, as said below
Outputs:
- result: float32 [8, 1024, 768], P('dp', 'seq')
- hidden_grad: float32 [8, 1024, 768], P('dp', 'seq')
- gating_grad: float32 [768, 1536], P(('dp', 'seq'), 'tensor')
- values_grad: float32 [768, 1536], P(('dp', 'seq'), 'tensor')
- selector_grad: float32 [768, 256], P(('dp', 'seq'), 'tensor')
- timestep_grad: float32 [768, 24], P(('dp', 'seq'), 'tensor')
- output_grad: float32 [1536, 768], P('tensor', ('dp', 'seq'))
- prenorm_grad: float32 [768], P(('dp', 'seq'))
- postnorm_grad: float32 [1536], P('tensor')
- filters_grad: float32 [5, 1536], P(None, 'tensor')
- kernels_grad: float32 [5, 256], P(None, 'tensor')
- scalars_grad: float32 [3, 24], P(None, 'tensor')
- gating_next: float32 [768, 1536], P(('dp', 'seq'), 'tensor')
- values_next: float32 [768, 1536], P(('dp', 'seq'), 'tensor')
- selector_next: float32 [768, 256], P(('dp', 'seq'), 'tensor')
- timestep_next: float32 [768, 24], P(('dp', 'seq'), 'tensor')
- output_next: float32 [1536, 768], P('tensor', ('dp', 'seq'))
- prenorm_next: float32 [768], P(('dp', 'seq'))
- postnorm_next: float32 [1536], P('tensor')
- filters_next: float32 [5, 1536], P(None, 'tensor')
- kernels_next: float32 [5, 256], P(None, 'tensor')
- scalars_next: float32 [3, 24], P(None, 'tensor')
- gating_state: float32 [2, 768, 1536], P(None, ('dp', 'seq'), 'tensor')
- values_state: float32 [2, 768, 1536], P(None, ('dp', 'seq'), 'tensor')
- selector_state: float32 [2, 768, 256], P(None, ('dp', 'seq'), 'tensor')
- timestep_state: float32 [2, 768, 24], P(None, ('dp', 'seq'), 'tensor')
- output_state: float32 [2, 1536, 768], P(None, 'tensor', ('dp', 'seq'))
- prenorm_state: float32 [2, 768], P(None, ('dp', 'seq'))
- postnorm_state: float32 [2, 1536], P(None, 'tensor')
- filters_state: float32 [2, 5, 1536], P(None, None, 'tensor')
- kernels_state: float32 [2, 5, 256], P(None, None, 'tensor')
- scalars_state: float32 [2, 3, 24], P(None, None, 'tensor')
The draws below stay inside these ranges and needn't reach their ends.
Inputs may be any that keep to these rules, and one draw needn't show every extreme that they name: `gating_adam`: index 1 is positive. `values_adam`: index 1 is positive. `selector_adam`: index 1 is positive. `timestep_adam`: index 1 is positive. `output_adam`: index 1 is positive. `prenorm_adam`: index 1 is positive. `postnorm_adam`: index 1 is positive. `filters_adam`: index 1 is positive. `kernels_adam`: index 1 is positive. `scalars_adam`: index 1 is positive.
All inputs are finite; a program needn't handle non-finite values.
Results may differ from the reference program's by a relative error of at most 0.015.
The reference program's roundings to bfloat16 on the way count: a program that leaves them out, or rounds other values in their place, can miss the bound.
Values may be sent and summed in bfloat16 or wider, within the bound.
A program may use at most 128 MiB of HBM per device.

```python
import math
import jax
import jax.numpy as jnp
from jax import lax

D = 768
INNER = 1536
STATE = 128
HEADDIM = 64
KCONV = 4
GROUP = 256
STEP = 2
HEADS = 24
SEQS = 8
LENGTH = 1024
N_SEQ = 4


def moment_pair(key, shape):
    first_key, second_key = jax.random.split(key)
    first = 0.4 * jnp.clip(jax.random.normal(first_key, shape, jnp.float32), -4.0, 4.0)
    second = 0.016 * jnp.exp(jax.random.uniform(second_key, shape, jnp.float32, -1.2, 1.2))
    return jnp.stack([first, second])


def draw_scalars(key, part):
    keys = jax.random.split(jax.random.fold_in(key, 7), 5)
    log_rate = jax.random.uniform(keys[0], (HEADS,), jnp.float32, 0.0, math.log(4.0))
    rate = jnp.exp(log_rate)
    slow_share = 0.5
    skip_top = 1.5
    slow = jax.random.uniform(keys[1], (HEADS,), jnp.float32) < slow_share
    reach = jnp.exp(jax.random.uniform(keys[2], (HEADS,), jnp.float32, math.log(0.3), math.log(0.6 * N_SEQ))) / (rate * LENGTH)
    quick = jnp.exp(jax.random.uniform(keys[3], (HEADS,), jnp.float32, math.log(0.02), math.log(0.07))) / rate
    delta = jnp.where(slow, reach, quick) * math.exp(-2.0)
    bias = jnp.log(jnp.expm1(delta))
    skip = jax.random.uniform(keys[4], (HEADS,), jnp.float32, 0.5, skip_top)
    return jnp.stack([bias, log_rate, skip])


def draw_gating_adam(key, part):
    return moment_pair(jax.random.fold_in(key, 101), (D, INNER))


def draw_values_adam(key, part):
    return moment_pair(jax.random.fold_in(key, 102), (D, INNER))


def draw_selector_adam(key, part):
    return moment_pair(jax.random.fold_in(key, 103), (D, 2 * STATE))


def draw_timestep_adam(key, part):
    return moment_pair(jax.random.fold_in(key, 104), (D, HEADS))


def draw_output_adam(key, part):
    return moment_pair(jax.random.fold_in(key, 105), (INNER, D))


def draw_prenorm_adam(key, part):
    magnitude = math.sqrt(SEQS * LENGTH)
    first_key, second_key = jax.random.split(jax.random.fold_in(key, 106))
    first = 0.15 * magnitude * jnp.clip(jax.random.normal(first_key, (D,), jnp.float32), -4.0, 4.0)
    second = 0.0017 * magnitude * magnitude * jnp.exp(jax.random.uniform(second_key, (D,), jnp.float32, -1.2, 1.2))
    return jnp.stack([first, second])


def draw_postnorm_adam(key, part):
    return moment_pair(jax.random.fold_in(key, 107), (INNER,))


def draw_filters_adam(key, part):
    return moment_pair(jax.random.fold_in(key, 108), (KCONV + 1, INNER))


def draw_kernels_adam(key, part):
    return moment_pair(jax.random.fold_in(key, 109), (KCONV + 1, 2 * STATE))


def draw_scalars_adam(key, part):
    return moment_pair(jax.random.fold_in(key, 110), (3, HEADS))


def level_of(rng, extent, cuts, smallest, high):
    loudness = 1.0
    for position, parts in cuts:
        heights = jax.random.uniform(jax.random.fold_in(jax.random.fold_in(rng, 6), position), (parts,), jnp.float32, smallest / len(cuts), high / len(cuts))
        loudness = loudness * jnp.repeat(jnp.exp(heights), extent[position] // parts).reshape((-1,) + (1,) * (len(extent) - 1 - position))
    return loudness


def bell_draw(rng, extent, width, limit, cuts=(), held_as=jnp.bfloat16):
    loudness = level_of(rng, extent, cuts, -0.22, 0.18) if cuts else 1.0
    values = jax.random.normal(rng, extent, jnp.float32) * width * loudness
    return jnp.minimum(jnp.maximum(values, -limit), limit).astype(held_as)


def setup_inputs(seed: int = 0) -> dict:
    key_of = jax.random.split(jax.random.key(seed), 23)
    return {
        "hidden": bell_draw(key_of[0], (SEQS, LENGTH, D), 1.0, 6.0, ((0, 4), (1, 4))),
        "cotangent": bell_draw(key_of[1], (SEQS, LENGTH, D), 1.0, 6.0, ((0, 4), (1, 4))),
        "gating": bell_draw(key_of[2], (D, INNER), D ** -0.5, 0.21875, ((0, 16), (1, 2)), jnp.float32),
        "values": bell_draw(key_of[3], (D, INNER), D ** -0.5, 0.21875, ((0, 16), (1, 2)), jnp.float32),
        "selector": bell_draw(key_of[4], (D, 2 * STATE), D ** -0.5, 0.21875, ((0, 16), (1, 2)), jnp.float32),
        "timestep": bell_draw(key_of[5], (D, HEADS), (D // 4) ** -0.5, 0.4375, ((0, 16), (1, 2)), jnp.float32),
        "output": bell_draw(key_of[6], (INNER, D), INNER ** -0.5, 0.15625, ((0, 2), (1, 16)), jnp.float32),
        "prenorm": jnp.clip(1.0 + 0.1 * jax.random.normal(key_of[7], (D,), jnp.float32), 0.5, 1.5),
        "postnorm": jnp.clip(1.0 + 0.1 * jax.random.normal(key_of[8], (INNER,), jnp.float32), 0.5, 1.5),
        "filters": bell_draw(key_of[9], (KCONV + 1, INNER), KCONV ** -0.5, 3.0, ((1, 2),), jnp.float32),
        "kernels": bell_draw(key_of[10], (KCONV + 1, 2 * STATE), KCONV ** -0.5, 3.0, ((1, 2),), jnp.float32),
        "scalars": draw_scalars(jax.random.fold_in(key_of[22], 71), 0),
        "gating_adam": draw_gating_adam(jax.random.fold_in(key_of[22], 71), 0),
        "values_adam": draw_values_adam(jax.random.fold_in(key_of[22], 71), 0),
        "selector_adam": draw_selector_adam(jax.random.fold_in(key_of[22], 71), 0),
        "timestep_adam": draw_timestep_adam(jax.random.fold_in(key_of[22], 71), 0),
        "output_adam": draw_output_adam(jax.random.fold_in(key_of[22], 71), 0),
        "prenorm_adam": draw_prenorm_adam(jax.random.fold_in(key_of[22], 71), 0),
        "postnorm_adam": draw_postnorm_adam(jax.random.fold_in(key_of[22], 71), 0),
        "filters_adam": draw_filters_adam(jax.random.fold_in(key_of[22], 71), 0),
        "kernels_adam": draw_kernels_adam(jax.random.fold_in(key_of[22], 71), 0),
        "scalars_adam": draw_scalars_adam(jax.random.fold_in(key_of[22], 71), 0),
    }


epsilon = 1e-05
highest = lax.Precision.HIGHEST
learn_rate = 0.01
first_decay = 0.9
second_decay = 0.999
adam_epsilon = 1e-08
weight_decay = 0.1

def swish_parts(value):
    sigmoid = jax.nn.sigmoid(value)
    return (value * sigmoid, sigmoid * (1.0 + value * (1.0 - sigmoid)))

def product(form, left, right):
    return jnp.einsum(form, left.astype(jnp.float32), right.astype(jnp.float32), precision=highest)

def conv_apply(padded, taps):
    tap_count = taps.shape[0] - 1
    length = padded.shape[1] - tap_count + 1
    wide = padded.astype(jnp.float32)
    total = taps[tap_count] + taps[0] * wide[:, 0:length]
    for index in range(1, tap_count):
        total = total + taps[index] * wide[:, index:index + length]
    return total

def conv_back(padded, taps, grad_pre):
    tap_count = taps.shape[0] - 1
    length = grad_pre.shape[1]
    wide = padded.astype(jnp.float32)
    tap_rows = [lax.optimization_barrier(jnp.sum(grad_pre * wide[:, index:index + length], axis=(0, 1))) for index in range(tap_count)]
    tap_rows.append(lax.optimization_barrier(jnp.sum(grad_pre, axis=(0, 1))))
    grad_pad = jnp.zeros(padded.shape, jnp.float32)
    for index in range(tap_count):
        grad_pad = grad_pad + jnp.pad(taps[index] * grad_pre, ((0, 0), (index, tap_count - 1 - index), (0, 0)))
    return (jnp.stack(tap_rows), grad_pad)

def group_terms(inner, write_vec, read_vec, delta, running):
    length = inner.shape[1]
    scores = product('btn,bun->btu', read_vec, write_vec)
    causal = jnp.arange(length)[:, None] >= jnp.arange(length)[None, :]
    by_head = jnp.transpose(running, (0, 2, 1))
    gap = by_head[:, :, :, None] - by_head[:, :, None, :]
    decays = jnp.exp(jnp.where(causal, gap, -jnp.inf))
    step_head = jnp.transpose(delta, (0, 2, 1))
    mixing = scores[:, None] * decays * step_head[:, :, None, :]
    mixing_b = mixing.astype(jnp.bfloat16)
    within = product('bhtu,buhp->bthp', mixing_b, inner)
    inner_f = inner.astype(jnp.float32)
    weight_end = jnp.exp(running[:, -1:, :] - running) * delta
    local_state = product('bthp,btn->bhpn', inner_f * weight_end[..., None], write_vec)
    carry_decay = jnp.exp(running[:, -1, :])
    return (scores, decays, mixing_b, within, weight_end, local_state, carry_decay)

def group_back_first(inner, write_vec, read_vec, delta, running, skip, entering, grad_mixer, scores, decays, mixing_b):
    grad_half = grad_mixer.astype(jnp.bfloat16)
    inner_f = inner.astype(jnp.float32)
    skip_grad = lax.optimization_barrier(jnp.sum(grad_mixer * inner_f, axis=(0, 1, 3)))
    grad_inner = skip[None, None, :, None] * grad_mixer + product('bhtu,bthp->buhp', mixing_b, grad_half)
    grad_mix = product('bthp,buhp->bhtu', grad_half, inner)
    step_head = jnp.transpose(delta, (0, 2, 1))
    kernel = grad_mix * decays * scores[:, None]
    grad_delta = jnp.transpose(lax.optimization_barrier(jnp.sum(kernel, axis=2)), (0, 2, 1))
    weighted = kernel * step_head[:, :, None, :]
    grad_running = jnp.transpose(lax.optimization_barrier(jnp.sum(weighted, axis=3)) - lax.optimization_barrier(jnp.sum(weighted, axis=2)), (0, 2, 1))
    grad_scores = lax.optimization_barrier(jnp.sum(grad_mix * decays * step_head[:, :, None, :], axis=1))
    grad_read = product('btu,bun->btn', grad_scores, write_vec)
    grad_write = product('btu,btn->bun', grad_scores, read_vec)
    growth = jnp.exp(running)
    across = product('btn,bhpn->bthp', read_vec, entering)
    grad_running = grad_running + lax.optimization_barrier(jnp.sum(grad_mixer * across, axis=3)) * growth
    scaled = grad_mixer * growth[..., None]
    grad_read = grad_read + product('bthp,bhpn->btn', scaled, entering)
    pushed = product('bthp,btn->bhpn', scaled, read_vec)
    return (grad_inner, grad_delta, grad_running, grad_write, grad_read, skip_grad, pushed)

def group_back_second(inner, write_vec, delta, running, weight_end, entering, carry_decay, end_grad, grad_inner, grad_delta, grad_running, grad_write):
    inner_f = inner.astype(jnp.float32)
    decay_grad = lax.optimization_barrier(jnp.sum(end_grad * entering, axis=(2, 3)))
    end_extra = decay_grad * carry_decay
    grad_xw = product('bhpn,btn->bthp', end_grad, write_vec)
    grad_write = grad_write + product('bhpn,bthp->btn', end_grad, inner_f * weight_end[..., None])
    grad_inner = grad_inner + grad_xw * weight_end[..., None]
    grad_weight = lax.optimization_barrier(jnp.sum(grad_xw * inner_f, axis=3))
    grad_delta = grad_delta + grad_weight * jnp.exp(running[:, -1:, :] - running)
    spread = grad_weight * weight_end
    end_extra = end_extra + lax.optimization_barrier(jnp.sum(spread, axis=1))
    grad_running = grad_running - spread
    grad_running = jnp.concatenate([grad_running[:, :-1], grad_running[:, -1:] + end_extra[:, None]], axis=1)
    grad_log = jnp.flip(jnp.cumsum(jnp.flip(grad_running, 1), axis=1), 1)
    return (grad_inner, grad_delta, grad_write, grad_log)

def adamw(param, moments, grad):
    first = first_decay * moments[0] + (1.0 - first_decay) * grad
    second = second_decay * moments[1] + (1.0 - second_decay) * grad * grad
    first_hat = first / (1.0 - first_decay ** STEP)
    second_hat = second / (1.0 - second_decay ** STEP)
    fresh = param - learn_rate * (first_hat / (jnp.sqrt(second_hat) + adam_epsilon) + weight_decay * param)
    return (fresh, jnp.stack([first, second]))

def advance(state, item):
    return (item[0][:, None, None] * state + item[1], state)

def reference(hidden, cotangent, gating, values, selector, timestep, output, prenorm, postnorm, filters, kernels, scalars, gating_adam, values_adam, selector_adam, timestep_adam, output_adam, prenorm_adam, postnorm_adam, filters_adam, kernels_adam, scalars_adam):
    half = jnp.bfloat16
    single = jnp.float32
    gate_weight = gating.astype(half)
    value_weight = values.astype(half)
    select_weight = selector.astype(half)
    delta_weight = timestep.astype(half)
    out_weight = output.astype(half)
    entry_gain = prenorm.astype(half).astype(single)
    groups = LENGTH // GROUP
    lead = KCONV - 1
    bias = scalars[0]
    rate = -jnp.exp(scalars[1])
    skip = scalars[2]

    def one_sequence(carry, pair):
        tokens, upstream = pair
        residual = tokens.astype(single)
        entry_scale = lax.rsqrt(lax.optimization_barrier(jnp.mean(residual * residual, axis=-1, keepdims=True)) + epsilon)
        normed = (residual * entry_scale * entry_gain).astype(half)
        gate_raw = jnp.dot(normed, gate_weight, preferred_element_type=single).astype(half)
        inner_raw = jnp.dot(normed, value_weight, preferred_element_type=single).astype(half)
        select_raw = jnp.dot(normed, select_weight, preferred_element_type=single).astype(half)
        delta_raw = jnp.dot(normed, delta_weight, preferred_element_type=single)
        inner_pad = jnp.concatenate([jnp.zeros((lead, INNER), half), inner_raw], axis=0)[None]
        select_pad = jnp.concatenate([jnp.zeros((lead, 2 * STATE), half), select_raw], axis=0)[None]
        inner_value, inner_slope = swish_parts(conv_apply(inner_pad, filters)[0])
        select_value, select_slope = swish_parts(conv_apply(select_pad, kernels)[0])
        inner_act = inner_value.astype(half)
        select_act = select_value.astype(half)
        delta = jax.nn.softplus(delta_raw + bias)
        inner_h = inner_act.reshape(groups, GROUP, HEADS, HEADDIM)
        write_vec = select_act[:, :STATE].reshape(groups, GROUP, STATE)
        read_vec = select_act[:, STATE:].reshape(groups, GROUP, STATE)
        delta_c = delta.reshape(groups, GROUP, HEADS)
        running = jnp.cumsum(delta_c * rate, axis=1)
        scores, decays, mixing_b, within, weight_end, local_state, carry_decay = group_terms(inner_h, write_vec, read_vec, delta_c, running)
        zeros = jnp.zeros((HEADS, HEADDIM, STATE), single)
        entering = lax.scan(advance, zeros, (carry_decay, local_state))[1]
        growth = jnp.exp(running)
        across = product('btn,bhpn->bthp', read_vec, entering)
        inner_f = inner_h.astype(single)
        mixer_out = (within + growth[..., None] * across + skip[None, None, :, None] * inner_f).reshape(LENGTH, INNER)
        gate_act, gate_slope = swish_parts(gate_raw.astype(single))
        gated = mixer_out * gate_act
        gate_scale = lax.rsqrt(lax.optimization_barrier(jnp.mean(gated * gated, axis=-1, keepdims=True)) + epsilon)
        mixed = (gated * gate_scale * postnorm).astype(half)
        result = residual + jnp.dot(mixed, out_weight, preferred_element_type=single)
        grad_mixed = jnp.dot(upstream, out_weight.T, preferred_element_type=single)
        output_grad = jnp.dot(mixed.T, upstream, preferred_element_type=single)
        postnorm_grad = lax.optimization_barrier(jnp.sum(grad_mixed * gated * gate_scale, axis=0))
        hat_gated = grad_mixed * postnorm
        cube = gate_scale * gate_scale * gate_scale
        grad_gated = gate_scale * hat_gated - gated * cube * lax.optimization_barrier(jnp.mean(hat_gated * gated, axis=-1, keepdims=True))
        grad_mixer = (grad_gated * gate_act).reshape(groups, GROUP, HEADS, HEADDIM)
        grad_gate = (grad_gated * mixer_out * gate_slope).astype(half)
        grad_inner, grad_delta, grad_running, grad_write, grad_read, skip_grad, pushed = group_back_first(inner_h, write_vec, read_vec, delta_c, running, skip, entering, grad_mixer, scores, decays, mixing_b)
        end_grad = lax.scan(advance, zeros, (carry_decay, pushed), reverse=True)[1]
        grad_inner, grad_delta, grad_write, grad_log = group_back_second(inner_h, write_vec, delta_c, running, weight_end, entering, carry_decay, end_grad, grad_inner, grad_delta, grad_running, grad_write)
        grad_delta = grad_delta + grad_log * rate
        alog_grad = lax.optimization_barrier(jnp.sum(grad_log * delta_c, axis=(0, 1))) * rate
        grad_delta_pre = grad_delta.reshape(LENGTH, HEADS) * jax.nn.sigmoid(delta_raw + bias)
        bias_grad = lax.optimization_barrier(jnp.sum(grad_delta_pre, axis=0))
        grad_select = jnp.concatenate([grad_write, grad_read], axis=2).reshape(LENGTH, 2 * STATE)
        filters_grad, inner_pad_grad = conv_back(inner_pad, filters, (grad_inner.reshape(LENGTH, INNER) * inner_slope)[None])
        kernels_grad, select_pad_grad = conv_back(select_pad, kernels, (grad_select * select_slope)[None])
        inner_raw_grad = inner_pad_grad[0, lead:].astype(half)
        select_raw_grad = select_pad_grad[0, lead:].astype(half)
        delta_half = grad_delta_pre.astype(half)
        grad_normed = jnp.dot(grad_gate, gate_weight.T, preferred_element_type=single)
        grad_normed = grad_normed + jnp.dot(inner_raw_grad, value_weight.T, preferred_element_type=single)
        grad_normed = grad_normed + jnp.dot(select_raw_grad, select_weight.T, preferred_element_type=single)
        grad_normed = grad_normed + jnp.dot(delta_half, delta_weight.T, preferred_element_type=single)
        prenorm_grad = lax.optimization_barrier(jnp.sum(grad_normed * residual * entry_scale, axis=0))
        hat = grad_normed * entry_gain
        hidden_grad = upstream.astype(single) + entry_scale * hat - residual * entry_scale * entry_scale * entry_scale * lax.optimization_barrier(jnp.mean(hat * residual, axis=-1, keepdims=True))
        terms = (jnp.dot(normed.T, grad_gate, preferred_element_type=single), jnp.dot(normed.T, inner_raw_grad, preferred_element_type=single), jnp.dot(normed.T, select_raw_grad, preferred_element_type=single), jnp.dot(normed.T, delta_half, preferred_element_type=single), output_grad, prenorm_grad, postnorm_grad, filters_grad, kernels_grad, jnp.stack([bias_grad, alog_grad, skip_grad]))
        carry = tuple((total + term for total, term in zip(carry, terms)))
        return (carry, (result, hidden_grad))
    params = (gating, values, selector, timestep, output, prenorm, postnorm, filters, kernels, scalars)
    moments = (gating_adam, values_adam, selector_adam, timestep_adam, output_adam, prenorm_adam, postnorm_adam, filters_adam, kernels_adam, scalars_adam)
    start = tuple((jnp.zeros(param.shape, single) for param in params))
    grads, stacked = lax.scan(one_sequence, start, (hidden, cotangent))
    updated = [adamw(param, moment, grad) for param, moment, grad in zip(params, moments, grads)]
    return (stacked[0], stacked[1], grads[0], grads[1], grads[2], grads[3], grads[4], grads[5], grads[6], grads[7], grads[8], grads[9], updated[0][0], updated[1][0], updated[2][0], updated[3][0], updated[4][0], updated[5][0], updated[6][0], updated[7][0], updated[8][0], updated[9][0], updated[0][1], updated[1][1], updated[2][1], updated[3][1], updated[4][1], updated[5][1], updated[6][1], updated[7][1], updated[8][1], updated[9][1])
```

```python
import functools
import jax
import jax.numpy as jnp
from jax import lax
from jax.experimental import pallas as pl
from jax.experimental.pallas import tpu as pltpu
from jax.sharding import PartitionSpec as P

INNER = 1536
STATE = 128
HEADDIM = 64
STEP = 2


epsilon = 1e-05
highest = lax.Precision.HIGHEST
learn_rate = 0.01
first_decay = 0.9
second_decay = 0.999
adam_epsilon = 1e-08
weight_decay = 0.1


def from_behind(block, axis, distance):
    devices = range(lax.axis_size(axis))
    route = [(i - distance, i) for i in devices if i - distance in devices]
    return lax.ppermute(block, axis, route)


MESH = pl.DeviceIdType.MESH
VMEM = pl.BlockSpec(memory_space=pltpu.VMEM)
ANY = pl.BlockSpec(memory_space=pl.ANY)


def send(src, dst, send_sem, recv_sem, device):
    return pltpu.make_async_remote_copy(
        src_ref=src,
        dst_ref=dst,
        send_sem=send_sem,
        recv_sem=recv_sem,
        device_id=device,
        device_id_type=MESH,
    )


def greet(devices):
    barrier = pltpu.get_barrier_semaphore()
    for device in devices:
        pl.semaphore_signal(barrier, inc=1, device_id=device, device_id_type=MESH)
    pl.semaphore_wait(barrier, len(devices))


def params_of(collective_id):
    return pltpu.CompilerParams(collective_id=collective_id, has_side_effects=True)


def swap_kernel(x_ref, o_ref, send_sem, recv_sem):
    other = {"tensor": 1 - lax.axis_index("tensor")}
    greet([other])
    copy = send(x_ref, o_ref, send_sem, recv_sem, other)
    copy.start()
    copy.wait()


def swap(value, collective_id):
    return pl.pallas_call(
        swap_kernel,
        out_shape=jax.ShapeDtypeStruct(value.shape, value.dtype),
        in_specs=[VMEM],
        out_specs=VMEM,
        scratch_shapes=[pltpu.SemaphoreType.DMA, pltpu.SemaphoreType.DMA],
        compiler_params=params_of(collective_id),
    )(value)


def carry_kernel(count, step, parts, decay_ref, local_ref, o_ref, out_buf, in_buf, send_sem, recv_sem):
    me = lax.axis_index("seq")
    target = lax.rem(me + count + step, count)
    source = lax.rem(me + count - step, count)
    first, last = (0, count - 1) if step > 0 else (count - 1, 0)
    greet([{"seq": target}, {"seq": source}])
    size = local_ref.shape[0] // parts

    def copy_of(part):
        return send(
            out_buf.at[part],
            in_buf.at[part],
            send_sem.at[part],
            recv_sem.at[part],
            {"seq": target},
        )

    for part in range(parts):
        rows = pl.ds(part * size, size)

        @pl.when(me == first)
        def _():
            o_ref[rows] = jnp.zeros((size,) + o_ref.shape[1:], o_ref.dtype)
            out_buf[part] = local_ref[rows].astype(jnp.bfloat16)

        @pl.when(me != first)
        def _():
            copy_of(part).wait_recv()
            entering = in_buf[part]
            o_ref[rows] = entering
            out_buf[part] = (
                decay_ref[rows] * entering.astype(jnp.float32) + local_ref[rows]
            ).astype(jnp.bfloat16)

        @pl.when(me != last)
        def _():
            copy_of(part).start()

    @pl.when(me != last)
    def _():
        for part in range(parts):
            copy_of(part).wait_send()


def carry(decay, local, count, step, collective_id):
    seqs, heads, wide, deep = local.shape
    total = seqs * heads
    parts = 6 if total % 6 == 0 else 1
    size = total // parts
    spread = jnp.broadcast_to(decay.reshape(total, 1, 1), (total, 1, deep))
    result = pl.pallas_call(
        functools.partial(carry_kernel, count, step, parts),
        out_shape=jax.ShapeDtypeStruct((total, wide, deep), jnp.bfloat16),
        in_specs=[VMEM, VMEM],
        out_specs=VMEM,
        scratch_shapes=[
            pltpu.VMEM((parts, size, wide, deep), jnp.bfloat16),
            pltpu.VMEM((parts, size, wide, deep), jnp.bfloat16),
            pltpu.SemaphoreType.DMA((parts,)),
            pltpu.SemaphoreType.DMA((parts,)),
        ],
        compiler_params=params_of(collective_id),
    )(spread, local.reshape(total, wide, deep))
    return result.reshape(local.shape)


def gather_kernel(n, x_ref, o_ref, own_sem, zs, zr, xs, xr, ys, yr, fxs, fxr, fys, fyr):
    d, s = lax.axis_index("dp"), lax.axis_index("seq")
    y, x = d // 2, lax.rem(d, 2)
    xn, yn = y * 2 + (1 - x), (1 - y) * 2 + x
    zt = [lax.rem(s + k, n) for k in range(n)]
    zf = [lax.rem(s + n - k, n) for k in range(n)]
    greet([{"seq": zt[k]} for k in range(1, n)] + [{"dp": xn}, {"dp": yn}])
    h = x_ref.shape[1] // 2
    own = pltpu.make_async_copy(x_ref, o_ref.at[d, s], own_sem)
    own.start()
    pend, xc, yc, fx, fy = [], [], [], [], []
    zc = []
    for k in range(1, n):
        copy = send(x_ref, o_ref.at[d, s], zs.at[k - 1], zr.at[k - 1], {"seq": zt[k]})
        zc.append(copy)

    def forward(j):
        z = zf[j]
        xc[j].wait_recv()
        copy = send(
            o_ref.at[xn, z, :, pl.ds(0, h)],
            o_ref.at[xn, z, :, pl.ds(0, h)],
            fys.at[j],
            fyr.at[j],
            {"dp": yn},
        )
        copy.start()
        fy.append(copy)
        yc[j].wait_recv()
        copy = send(
            o_ref.at[yn, z, :, pl.ds(h, h)],
            o_ref.at[yn, z, :, pl.ds(h, h)],
            fxs.at[j],
            fxr.at[j],
            {"dp": xn},
        )
        copy.start()
        fx.append(copy)

    for j in range(n):
        z = zf[j]
        if j:
            zc[j - 1].wait_recv()
        block = x_ref if j == 0 else o_ref.at[d, z]
        copy = send(block, o_ref.at[d, z], xs.at[j], xr.at[j], {"dp": xn})
        copy.start()
        xc.append(copy)
        copy = send(block, o_ref.at[d, z], ys.at[j], yr.at[j], {"dp": yn})
        copy.start()
        yc.append(copy)
        if j == 0:
            for copy in zc:
                copy.start()
        else:
            forward(j - 1)
    forward(n - 1)
    for copy in fx + fy:
        copy.wait_recv()
    for copy in zc + xc + yc + fx + fy:
        copy.wait_send()
    own.wait()


def gather(packed, n):
    rows, columns = packed.shape
    dma = pltpu.SemaphoreType.DMA
    return pl.pallas_call(
        functools.partial(gather_kernel, n),
        out_shape=jax.ShapeDtypeStruct((4, n, rows, columns), packed.dtype),
        in_specs=[VMEM],
        out_specs=ANY,
        scratch_shapes=[dma, dma((n - 1,)), dma((n - 1,))] + [dma((n,))] * 8,
        compiler_params=params_of(0),
    )(packed).reshape(4 * n * rows, columns)


def reduce_kernel(
    n, g_ref, small_ref, o_ref, small_o,
    rxa, rya, ryb, rxb, ta, tb, zb, zin, zsmall, dsmall,
    s1, r1, s2, r2, s3, r3, s4, r4, s5, r5, s6, r6, s7, r7,
):
    d, s = lax.axis_index("dp"), lax.axis_index("seq")
    y, x = d // 2, lax.rem(d, 2)
    xn, yn = {"dp": y * 2 + (1 - x)}, {"dp": (1 - y) * 2 + x}
    zt = [lax.rem(s + k, n) for k in range(n)]
    others = [{"dp": lax.rem(d + k, 4)} for k in range(1, 4)]
    greet([{"seq": zt[k]} for k in range(1, n)] + others)
    h = g_ref.shape[4] // 2
    left, right = pl.ds(0, h), pl.ds(h, h)
    single, half = jnp.float32, jnp.bfloat16
    order = list(range(1, n)) + [0]
    smalls = []
    for k in range(1, n):
        copy = send(small_ref, zsmall.at[s], s6.at[k - 1], r6.at[k - 1], {"seq": zt[k]})
        copy.start()
        smalls.append(copy)
    a1, b1, a2, b2, z1 = {}, {}, {}, {}, {}
    for j in order:
        a1[j] = send(g_ref.at[:, 1 - x, zt[j], :, left], rxa.at[j], s1.at[j], r1.at[j], xn)
        a1[j].start()
        b1[j] = send(g_ref.at[1 - y, :, zt[j], :, right], ryb.at[j], s2.at[j], r2.at[j], yn)
        b1[j].start()
    zsmall[s] = small_ref[...]
    for copy in smalls:
        copy.wait_recv()
    total = zsmall[0]
    for k in range(1, n):
        total = total + zsmall[k]
    dsmall[d] = total
    widely = []
    for k in range(3):
        copy = send(dsmall.at[d], dsmall.at[d], s7.at[k], r7.at[k], others[k])
        copy.start()
        widely.append(copy)

    def middle(j):
        z = zt[j]
        a1[j].wait_recv()
        ta[j] = (
            g_ref[1 - y, x, z, :, left].astype(single) + rxa[j, 1 - y].astype(single)
        ).astype(half)
        a2[j] = send(ta.at[j], rya.at[j], s3.at[j], r3.at[j], yn)
        a2[j].start()
        b1[j].wait_recv()
        tb[j] = (
            g_ref[y, 1 - x, z, :, right].astype(single) + ryb[j, 1 - x].astype(single)
        ).astype(half)
        b2[j] = send(tb.at[j], rxb.at[j], s4.at[j], r4.at[j], xn)
        b2[j].start()

    def finish(j):
        z = zt[j]
        a2[j].wait_recv()
        low = (
            g_ref[y, x, z, :, left].astype(single)
            + rxa[j, y].astype(single)
            + rya[j].astype(single)
        )
        b2[j].wait_recv()
        high = (
            g_ref[y, x, z, :, right].astype(single)
            + ryb[j, x].astype(single)
            + rxb[j].astype(single)
        )
        if j == 0:
            o_ref[:, left] = low
            o_ref[:, right] = high
        else:
            zb[j - 1, :, left] = low.astype(half)
            zb[j - 1, :, right] = high.astype(half)
            z1[j] = send(
                zb.at[j - 1], zin.at[j - 1], s5.at[j - 1], r5.at[j - 1], {"seq": zt[j]}
            )
            z1[j].start()

    for place, j in enumerate(order):
        middle(j)
        if place:
            finish(order[place - 1])
    finish(0)
    for copy in widely:
        copy.wait_recv()
    small_o[...] = dsmall[0] + dsmall[1] + dsmall[2] + dsmall[3]
    for j in range(1, n):
        z1[j].wait_recv()
        o_ref[...] = o_ref[...] + zin[j - 1].astype(single)
    for copy in smalls + widely:
        copy.wait_send()
    for group in (a1, b1, a2, b2, z1):
        for copy in group.values():
            copy.wait_send()


def reduce(grads, small, n):
    rows, columns = grads.shape[0] // (4 * n), grads.shape[1]
    h = columns // 2
    half = jnp.bfloat16
    dma = pltpu.SemaphoreType.DMA
    block = pltpu.VMEM((n, rows, h), half)
    double = pltpu.VMEM((n, 2, rows, h), half)
    row = pltpu.VMEM((n - 1, rows, columns), half)
    sems = [dma((n,))] * 8 + [dma((n - 1,))] * 4 + [dma((3,))] * 2
    return pl.pallas_call(
        functools.partial(reduce_kernel, n),
        out_shape=(
            jax.ShapeDtypeStruct((rows, columns), jnp.float32),
            jax.ShapeDtypeStruct(small.shape, jnp.float32),
        ),
        in_specs=[VMEM, VMEM],
        out_specs=(VMEM, VMEM),
        scratch_shapes=[double, block, double, block, block, block, row, row]
        + [
            pltpu.VMEM((n,) + small.shape, jnp.float32),
            pltpu.VMEM((4,) + small.shape, jnp.float32),
        ]
        + sems,
        compiler_params=params_of(9),
    )(grads.reshape(2, 2, n, rows, columns), small)


def swish_parts(value):
    sigmoid = jax.nn.sigmoid(value)
    return (value * sigmoid, sigmoid * (1.0 + value * (1.0 - sigmoid)))


def conv_apply(padded, taps):
    tap_count = taps.shape[0] - 1
    length = padded.shape[1] - tap_count + 1
    wide = padded.astype(jnp.float32)
    total = taps[tap_count] + taps[0] * wide[:, 0:length]
    for index in range(1, tap_count):
        total = total + taps[index] * wide[:, index : index + length]
    return total


def conv_back(padded, taps, grad_pre):
    tap_count = taps.shape[0] - 1
    length = grad_pre.shape[1]
    wide = padded.astype(jnp.float32)
    tap_rows = [
        jnp.sum(grad_pre * wide[:, index : index + length], axis=(0, 1))
        for index in range(tap_count)
    ]
    tap_rows.append(jnp.sum(grad_pre, axis=(0, 1)))
    grad_pad = jnp.zeros(padded.shape, jnp.float32)
    for index in range(tap_count):
        grad_pad = grad_pad + jnp.pad(
            taps[index] * grad_pre, ((0, 0), (index, tap_count - 1 - index), (0, 0))
        )
    return (jnp.stack(tap_rows), grad_pad)


def adamw(param, moments, grad):
    first = first_decay * moments[0] + (1.0 - first_decay) * grad
    second = second_decay * moments[1] + (1.0 - second_decay) * grad * grad
    first_hat = first / (1.0 - first_decay**STEP)
    second_hat = second / (1.0 - second_decay**STEP)
    fresh = param - learn_rate * (
        first_hat / (jnp.sqrt(second_hat) + adam_epsilon) + weight_decay * param
    )
    return (fresh, jnp.stack([first, second]))


def shards(
    hidden,
    cotangent,
    gating,
    values,
    selector,
    timestep,
    output,
    prenorm,
    postnorm,
    filters,
    kernels,
    scalars,
    gating_adam,
    values_adam,
    selector_adam,
    timestep_adam,
    output_adam,
    prenorm_adam,
    postnorm_adam,
    filters_adam,
    kernels_adam,
    scalars_adam,
):
    half = jnp.bfloat16
    single = jnp.float32
    n_dp, n_seq = lax.axis_size("dp"), lax.axis_size("seq")
    core = lax.axis_index("tensor")
    seqs_dev, length, width = hidden.shape
    rows = seqs_dev * length
    own_rows = gating.shape[0]
    lead = filters.shape[0] - 2
    heads_here = timestep.shape[1]
    inner_here = gating.shape[1]
    select_here = selector.shape[1]
    conv_end = 2 * inner_here + select_here
    step_wide = 128
    in_wide = conv_end + step_wide
    packed = jnp.concatenate(
        [
            gating.astype(half),
            values.astype(half),
            selector.astype(half),
            timestep.astype(half),
            prenorm.astype(half)[:, None],
            jnp.zeros((own_rows, step_wide - heads_here - 1), half),
            output.T.astype(half),
        ],
        axis=1,
    )
    if n_dp == 4:
        weights = gather(packed, n_seq)
    else:
        weights = lax.all_gather(packed, ("dp", "seq"), axis=0, tiled=True)
    in_weight = weights[:, :in_wide]
    out_weight = weights[:, in_wide:]
    bias = scalars[0]
    rate = -jnp.exp(scalars[1])
    skip = scalars[2]
    entry_gain = weights[:, conv_end + heads_here].astype(single)
    residual = hidden.astype(single)
    entry_scale = lax.rsqrt(jnp.mean(residual * residual, axis=-1, keepdims=True) + epsilon)
    normed = (residual * entry_scale * entry_gain).astype(half)
    flat = normed.reshape(rows, width)
    raw = jnp.dot(flat, in_weight, preferred_element_type=single)
    gate_raw = raw[:, :inner_here].astype(half).reshape(seqs_dev, length, inner_here)
    conv_raw = raw[:, inner_here:conv_end].astype(half).reshape(seqs_dev, length, -1)
    delta_raw = raw[:, conv_end : conv_end + heads_here].reshape(seqs_dev, length, heads_here)
    tails = from_behind(conv_raw[:, length - lead :], "seq", 1)
    conv_pad = jnp.concatenate([tails, conv_raw], axis=1)
    taps = jnp.concatenate([filters, kernels], axis=1)
    conv_value, conv_slope = swish_parts(conv_apply(conv_pad, taps))
    conv_act = conv_value.astype(half)
    inner_act = conv_act[:, :, :inner_here]
    mine = conv_act[:, :, inner_here:]
    theirs = swap(mine.reshape(rows, select_here), 1).reshape(mine.shape)
    write_vec = jnp.where(core == 0, mine, theirs)
    read_vec = jnp.where(core == 0, theirs, mine)
    delta = jax.nn.softplus(delta_raw + bias)
    running = jnp.cumsum(delta * rate, axis=1)
    inner_h = inner_act.reshape(seqs_dev, length, heads_here, HEADDIM)
    inner_f = inner_h.astype(single)
    weight_end = jnp.exp(running[:, -1:, :] - running) * delta
    carry_decay = jnp.exp(running[:, -1, :])
    growth = jnp.exp(running)
    inner_w = (inner_f * weight_end[..., None]).astype(half)
    local_state = jnp.einsum("bthp,btn->bhpn", inner_w, write_vec, preferred_element_type=single)
    entering = carry(carry_decay, local_state, n_seq, 1, 7)
    scores = jnp.einsum("btn,bun->btu", read_vec, write_vec, preferred_element_type=single)
    causal = jnp.arange(length)[:, None] >= jnp.arange(length)[None, :]
    by_head = jnp.transpose(running, (0, 2, 1))
    gap = by_head[:, :, :, None] - by_head[:, :, None, :]
    decays = jnp.exp(jnp.where(causal, gap, -jnp.inf))
    step_head = jnp.transpose(delta, (0, 2, 1))
    mixing_b = (scores[:, None] * decays * step_head[:, :, None, :]).astype(half)
    within = jnp.einsum("bhtu,buhp->bthp", mixing_b, inner_h, preferred_element_type=single)
    across = jnp.einsum("btn,bhpn->bthp", read_vec, entering, preferred_element_type=single)
    mixer_out = (within + growth[..., None] * across + skip[None, None, :, None] * inner_f).reshape(
        seqs_dev, length, inner_here
    )
    gate_act, gate_slope = swish_parts(gate_raw.astype(single))
    gated = mixer_out * gate_act
    upstream = cotangent.reshape(rows, width)
    grad_mixed = jnp.dot(upstream, out_weight, preferred_element_type=single).reshape(
        seqs_dev, length, inner_here
    )
    hat_gated = grad_mixed * postnorm
    sums = jnp.stack([jnp.sum(gated * gated, axis=-1), jnp.sum(hat_gated * gated, axis=-1)])
    lanes = sums.reshape(-1, 128)
    sums = (lanes + swap(lanes, 2)).reshape(sums.shape)
    squares, dots = sums[0], sums[1]
    gate_scale = lax.rsqrt(squares / INNER + epsilon)[..., None]
    mixed_flat = (gated * gate_scale * postnorm).astype(half).reshape(rows, inner_here)
    branch = lax.dot_general(
        mixed_flat, out_weight, (((1,), (1,)), ((), ())), preferred_element_type=single
    ).astype(half)
    branch = branch.astype(single) + swap(branch, 3).astype(single)
    result = residual + branch.reshape(seqs_dev, length, width)
    output_grad = lax.dot_general(
        upstream, mixed_flat, (((0,), (0,)), ((), ())), preferred_element_type=single
    )
    postnorm_grad = jnp.sum(grad_mixed * gated * gate_scale, axis=(0, 1))
    cube = gate_scale * gate_scale * gate_scale
    grad_gated = gate_scale * hat_gated - gated * cube * (dots / INNER)[..., None]
    grad_mixer = (grad_gated * gate_act).reshape(seqs_dev, length, heads_here, HEADDIM)
    grad_gate = (grad_gated * mixer_out * gate_slope).astype(half).reshape(rows, inner_here)

    scaled = (grad_mixer * growth[..., None]).astype(half)
    pushed = jnp.einsum("bthp,btn->bhpn", scaled, read_vec, preferred_element_type=single)
    end_grad = carry(carry_decay, pushed, n_seq, -1, 8)

    grad_half = grad_mixer.astype(half)
    skip_grad = jnp.sum(grad_mixer * inner_f, axis=(0, 1, 3))
    grad_inner = skip[None, None, :, None] * grad_mixer + jnp.einsum(
        "bhtu,bthp->buhp", mixing_b, grad_half, preferred_element_type=single
    )
    grad_mix = jnp.einsum("bthp,buhp->bhtu", grad_half, inner_h, preferred_element_type=single)
    spread_mix = grad_mix * decays
    kernel = spread_mix * scores[:, None]
    grad_delta = jnp.transpose(jnp.sum(kernel, axis=2), (0, 2, 1))
    weighted = kernel * step_head[:, :, None, :]
    grad_running = jnp.transpose(jnp.sum(weighted, axis=3) - jnp.sum(weighted, axis=2), (0, 2, 1))
    grad_scores = jnp.sum(spread_mix * step_head[:, :, None, :], axis=1).astype(half)
    grad_read = jnp.einsum("btu,bun->btn", grad_scores, write_vec, preferred_element_type=single)
    grad_write = jnp.einsum("btu,btn->bun", grad_scores, read_vec, preferred_element_type=single)
    grad_running = grad_running + jnp.sum(grad_mixer * across, axis=3) * growth
    grad_read = grad_read + jnp.einsum(
        "bthp,bhpn->btn", scaled, entering, preferred_element_type=single
    )

    decay_grad = jnp.sum(end_grad.astype(single) * entering.astype(single), axis=(2, 3))
    end_extra = decay_grad * carry_decay
    grad_xw = jnp.einsum("bhpn,btn->bthp", end_grad, write_vec, preferred_element_type=single)
    grad_write = grad_write + jnp.einsum(
        "bhpn,bthp->btn", end_grad, inner_w, preferred_element_type=single
    )
    grad_inner = grad_inner + grad_xw * weight_end[..., None]
    grad_weight = jnp.sum(grad_xw * inner_f, axis=3)
    grad_delta = grad_delta + grad_weight * jnp.exp(running[:, -1:, :] - running)
    spread = grad_weight * weight_end
    end_extra = end_extra + jnp.sum(spread, axis=1)
    grad_running = grad_running - spread
    grad_running = jnp.concatenate(
        [grad_running[:, :-1], grad_running[:, -1:] + end_extra[:, None]], axis=1
    )
    grad_log = jnp.flip(jnp.cumsum(jnp.flip(grad_running, 1), axis=1), 1)

    grad_delta = grad_delta + grad_log * rate
    alog_grad = jnp.sum(grad_log * delta, axis=(0, 1)) * rate
    grad_delta_pre = grad_delta * jax.nn.sigmoid(delta_raw + bias)
    bias_grad = jnp.sum(grad_delta_pre, axis=(0, 1))
    kept = jnp.where(core == 0, grad_write, grad_read)
    given = jnp.where(core == 0, grad_read, grad_write)
    grad_select = kept + swap(given.reshape(rows, select_here), 4).reshape(kept.shape)
    grad_conv = jnp.concatenate(
        [grad_inner.reshape(seqs_dev, length, inner_here), grad_select], axis=2
    )
    taps_grad, conv_pad_grad = conv_back(conv_pad, taps, grad_conv * conv_slope)
    back = from_behind(conv_pad_grad[:, :lead], "seq", -1)
    conv_raw_grad = (
        jnp.concatenate(
            [conv_pad_grad[:, lead:length], conv_pad_grad[:, length:] + back], axis=1
        )
        .astype(half)
        .reshape(rows, -1)
    )
    grad_all = jnp.concatenate(
        [
            grad_gate,
            conv_raw_grad,
            grad_delta_pre.astype(half).reshape(rows, heads_here),
            jnp.zeros((rows, step_wide - heads_here), half),
        ],
        axis=1,
    )
    grad_part = lax.dot_general(
        grad_all, in_weight, (((1,), (1,)), ((), ())), preferred_element_type=single
    ).astype(half)
    grad_part = grad_part.astype(single) + swap(grad_part, 5).astype(single)
    grad_normed = grad_part.reshape(seqs_dev, length, width)
    in_grad = lax.dot_general(
        flat, grad_all, (((0,), (0,)), ((), ())), preferred_element_type=single
    )
    prenorm_grad = jnp.sum(grad_normed * residual * entry_scale, axis=(0, 1))
    hat = grad_normed * entry_gain
    hidden_grad = (
        cotangent.astype(single)
        + entry_scale * hat
        - residual
        * entry_scale
        * entry_scale
        * entry_scale
        * jnp.mean(hat * residual, axis=-1, keepdims=True)
    )
    gain_column = conv_end + heads_here
    packed_grad = jnp.concatenate(
        [
            in_grad[:, :gain_column].astype(half),
            prenorm_grad.astype(half)[:, None],
            in_grad[:, gain_column + 1 :].astype(half),
            output_grad.astype(half),
        ],
        axis=1,
    )
    tap_rows = filters.shape[0]
    scalars_local = jnp.stack([bias_grad, alog_grad, skip_grad])
    loose = jnp.concatenate([taps_grad[:, inner_here:].reshape(-1), scalars_local.reshape(-1)])
    small = jnp.concatenate(
        [
            taps_grad[:, :inner_here],
            postnorm_grad[None],
            jnp.pad(loose, (0, inner_here - loose.shape[0]))[None],
            jnp.zeros((8 - tap_rows - 2, inner_here), single),
        ],
        axis=0,
    )
    if n_dp == 4:
        summed, small = reduce(packed_grad, small, n_seq)
    else:
        summed = lax.psum_scatter(
            packed_grad.astype(single), ("dp", "seq"), scatter_dimension=0, tiled=True
        )
        small = lax.psum(small, ("dp", "seq"))
    loose_end = tap_rows * select_here
    grads = (
        summed[:, :inner_here],
        summed[:, inner_here : 2 * inner_here],
        summed[:, 2 * inner_here : conv_end],
        summed[:, conv_end:gain_column],
        summed[:, in_wide:].T,
        summed[:, gain_column],
        small[tap_rows],
        small[:tap_rows],
        small[tap_rows + 1, :loose_end].reshape(tap_rows, select_here),
        small[tap_rows + 1, loose_end : loose_end + 3 * heads_here].reshape(3, heads_here),
    )
    params = (
        gating,
        values,
        selector,
        timestep,
        output,
        prenorm,
        postnorm,
        filters,
        kernels,
        scalars,
    )
    moments = (
        gating_adam,
        values_adam,
        selector_adam,
        timestep_adam,
        output_adam,
        prenorm_adam,
        postnorm_adam,
        filters_adam,
        kernels_adam,
        scalars_adam,
    )
    updated = [adamw(param, moment, grad) for param, moment, grad in zip(params, moments, grads)]
    return (
        result,
        hidden_grad,
        grads[0],
        grads[1],
        grads[2],
        grads[3],
        grads[4],
        grads[5],
        grads[6],
        grads[7],
        grads[8],
        grads[9],
        updated[0][0],
        updated[1][0],
        updated[2][0],
        updated[3][0],
        updated[4][0],
        updated[5][0],
        updated[6][0],
        updated[7][0],
        updated[8][0],
        updated[9][0],
        updated[0][1],
        updated[1][1],
        updated[2][1],
        updated[3][1],
        updated[4][1],
        updated[5][1],
        updated[6][1],
        updated[7][1],
        updated[8][1],
        updated[9][1],
    )


def solution(mesh):
    placed = (
        P("dp", "seq", None),
        P("dp", "seq", None),
        P(("dp", "seq"), "tensor"),
        P(("dp", "seq"), "tensor"),
        P(("dp", "seq"), "tensor"),
        P(("dp", "seq"), "tensor"),
        P("tensor", ("dp", "seq")),
        P(("dp", "seq")),
        P("tensor"),
        P(None, "tensor"),
        P(None, "tensor"),
        P(None, "tensor"),
        P(None, ("dp", "seq"), "tensor"),
        P(None, ("dp", "seq"), "tensor"),
        P(None, ("dp", "seq"), "tensor"),
        P(None, ("dp", "seq"), "tensor"),
        P(None, "tensor", ("dp", "seq")),
        P(None, ("dp", "seq")),
        P(None, "tensor"),
        P(None, None, "tensor"),
        P(None, None, "tensor"),
        P(None, None, "tensor"),
    )
    return jax.shard_map(
        shards,
        mesh=mesh,
        in_specs=placed,
        out_specs=(
            P("dp", "seq", None),
            P("dp", "seq", None),
            P(("dp", "seq"), "tensor"),
            P(("dp", "seq"), "tensor"),
            P(("dp", "seq"), "tensor"),
            P(("dp", "seq"), "tensor"),
            P("tensor", ("dp", "seq")),
            P(("dp", "seq")),
            P("tensor"),
            P(None, "tensor"),
            P(None, "tensor"),
            P(None, "tensor"),
            P(("dp", "seq"), "tensor"),
            P(("dp", "seq"), "tensor"),
            P(("dp", "seq"), "tensor"),
            P(("dp", "seq"), "tensor"),
            P("tensor", ("dp", "seq")),
            P(("dp", "seq")),
            P("tensor"),
            P(None, "tensor"),
            P(None, "tensor"),
            P(None, "tensor"),
            P(None, ("dp", "seq"), "tensor"),
            P(None, ("dp", "seq"), "tensor"),
            P(None, ("dp", "seq"), "tensor"),
            P(None, ("dp", "seq"), "tensor"),
            P(None, "tensor", ("dp", "seq")),
            P(None, ("dp", "seq")),
            P(None, "tensor"),
            P(None, None, "tensor"),
            P(None, None, "tensor"),
            P(None, None, "tensor"),
        ),
        check_vma=False,
    )
```

```python
import functools
import jax
import jax.numpy as jnp
from jax import lax
from jax.experimental import pallas as pl
from jax.experimental.pallas import tpu as pltpu
from jax.sharding import PartitionSpec as P

INNER = 1536
STATE = 128
HEADDIM = 64
STEP = 2


epsilon = 1e-05
highest = lax.Precision.HIGHEST
learn_rate = 0.01
first_decay = 0.9
second_decay = 0.999
adam_epsilon = 1e-08
weight_decay = 0.1


def from_behind(block, axis, distance):
    devices = range(lax.axis_size(axis))
    route = [(i - distance, i) for i in devices if i - distance in devices]
    return lax.ppermute(block, axis, route)


MESH = pl.DeviceIdType.MESH
VMEM = pl.BlockSpec(memory_space=pltpu.VMEM)
ANY = pl.BlockSpec(memory_space=pl.ANY)


def send(src, dst, send_sem, recv_sem, device):
    return pltpu.make_async_remote_copy(
        src_ref=src,
        dst_ref=dst,
        send_sem=send_sem,
        recv_sem=recv_sem,
        device_id=device,
        device_id_type=MESH,
    )


def greet(devices):
    barrier = pltpu.get_barrier_semaphore()
    for device in devices:
        pl.semaphore_signal(barrier, inc=1, device_id=device, device_id_type=MESH)
    pl.semaphore_wait(barrier, len(devices))


def params_of(collective_id):
    return pltpu.CompilerParams(collective_id=collective_id, has_side_effects=True)


def swap_kernel(x_ref, o_ref, send_sem, recv_sem):
    other = {"tensor": 1 - lax.axis_index("tensor")}
    greet([other])
    copy = send(x_ref, o_ref, send_sem, recv_sem, other)
    copy.start()
    copy.wait()


def swap(value, collective_id):
    return pl.pallas_call(
        swap_kernel,
        out_shape=jax.ShapeDtypeStruct(value.shape, value.dtype),
        in_specs=[VMEM],
        out_specs=VMEM,
        scratch_shapes=[pltpu.SemaphoreType.DMA, pltpu.SemaphoreType.DMA],
        compiler_params=params_of(collective_id),
    )(value)


def carry_kernel(count, step, parts, decay_ref, local_ref, o_ref, out_buf, in_buf, send_sem, recv_sem):
    me = lax.axis_index("seq")
    target = lax.rem(me + count + step, count)
    source = lax.rem(me + count - step, count)
    first, last = (0, count - 1) if step > 0 else (count - 1, 0)
    greet([{"seq": target}, {"seq": source}])
    size = local_ref.shape[0] // parts

    def copy_of(part):
        return send(
            out_buf.at[part],
            in_buf.at[part],
            send_sem.at[part],
            recv_sem.at[part],
            {"seq": target},
        )

    for part in range(parts):
        rows = pl.ds(part * size, size)

        @pl.when(me == first)
        def _():
            o_ref[rows] = jnp.zeros((size,) + o_ref.shape[1:], o_ref.dtype)
            out_buf[part] = local_ref[rows].astype(jnp.bfloat16)

        @pl.when(me != first)
        def _():
            copy_of(part).wait_recv()
            entering = in_buf[part]
            o_ref[rows] = entering
            out_buf[part] = (
                decay_ref[rows] * entering.astype(jnp.float32) + local_ref[rows]
            ).astype(jnp.bfloat16)

        @pl.when(me != last)
        def _():
            copy_of(part).start()

    @pl.when(me != last)
    def _():
        for part in range(parts):
            copy_of(part).wait_send()


def carry(decay, local, count, step, collective_id):
    seqs, heads, wide, deep = local.shape
    total = seqs * heads
    parts = 6 if total % 6 == 0 else 1
    size = total // parts
    spread = jnp.broadcast_to(decay.reshape(total, 1, 1), (total, 1, deep))
    result = pl.pallas_call(
        functools.partial(carry_kernel, count, step, parts),
        out_shape=jax.ShapeDtypeStruct((total, wide, deep), jnp.bfloat16),
        in_specs=[VMEM, VMEM],
        out_specs=VMEM,
        scratch_shapes=[
            pltpu.VMEM((parts, size, wide, deep), jnp.bfloat16),
            pltpu.VMEM((parts, size, wide, deep), jnp.bfloat16),
            pltpu.SemaphoreType.DMA((parts,)),
            pltpu.SemaphoreType.DMA((parts,)),
        ],
        compiler_params=params_of(collective_id),
    )(spread, local.reshape(total, wide, deep))
    return result.reshape(local.shape)


def gather_kernel(n, x_ref, o_ref, own_sem, zs, zr, xs, xr, ys, yr, fxs, fxr, fys, fyr):
    d, s = lax.axis_index("dp"), lax.axis_index("seq")
    y, x = d // 2, lax.rem(d, 2)
    xn, yn = y * 2 + (1 - x), (1 - y) * 2 + x
    zt = [lax.rem(s + k, n) for k in range(n)]
    zf = [lax.rem(s + n - k, n) for k in range(n)]
    greet([{"seq": zt[k]} for k in range(1, n)] + [{"dp": xn}, {"dp": yn}])
    h = x_ref.shape[1] // 2
    own = pltpu.make_async_copy(x_ref, o_ref.at[d, s], own_sem)
    own.start()
    pend, xc, yc, fx, fy = [], [], [], [], []
    zc = []
    for k in range(1, n):
        copy = send(x_ref, o_ref.at[d, s], zs.at[k - 1], zr.at[k - 1], {"seq": zt[k]})
        zc.append(copy)

    def forward(j):
        z = zf[j]
        xc[j].wait_recv()
        copy = send(
            o_ref.at[xn, z, :, pl.ds(0, h)],
            o_ref.at[xn, z, :, pl.ds(0, h)],
            fys.at[j],
            fyr.at[j],
            {"dp": yn},
        )
        copy.start()
        fy.append(copy)
        yc[j].wait_recv()
        copy = send(
            o_ref.at[yn, z, :, pl.ds(h, h)],
            o_ref.at[yn, z, :, pl.ds(h, h)],
            fxs.at[j],
            fxr.at[j],
            {"dp": xn},
        )
        copy.start()
        fx.append(copy)

    for j in range(n):
        z = zf[j]
        if j:
            zc[j - 1].wait_recv()
        block = x_ref if j == 0 else o_ref.at[d, z]
        copy = send(block, o_ref.at[d, z], xs.at[j], xr.at[j], {"dp": xn})
        copy.start()
        xc.append(copy)
        copy = send(block, o_ref.at[d, z], ys.at[j], yr.at[j], {"dp": yn})
        copy.start()
        yc.append(copy)
        if j == 0:
            for copy in zc:
                copy.start()
        else:
            forward(j - 1)
    forward(n - 1)
    for copy in fx + fy:
        copy.wait_recv()
    for copy in zc + xc + yc + fx + fy:
        copy.wait_send()
    own.wait()


def gather(packed, n):
    rows, columns = packed.shape
    dma = pltpu.SemaphoreType.DMA
    return pl.pallas_call(
        functools.partial(gather_kernel, n),
        out_shape=jax.ShapeDtypeStruct((4, n, rows, columns), packed.dtype),
        in_specs=[VMEM],
        out_specs=ANY,
        scratch_shapes=[dma, dma((n - 1,)), dma((n - 1,))] + [dma((n,))] * 8,
        compiler_params=params_of(0),
    )(packed).reshape(4 * n * rows, columns)


def reduce_kernel(
    n, g_ref, small_ref, u_ref, v_ref, o_ref, small_o, uo, vo,
    rxa, rya, ryb, rxb, ta, tb, zb, zin, zsmall, dsmall, tsmall, cs, cr,
    s1, r1, s2, r2, s3, r3, s4, r4, s5, r5, s6, r6, s7, r7,
):
    d, s = lax.axis_index("dp"), lax.axis_index("seq")
    y, x = d // 2, lax.rem(d, 2)
    xn, yn = {"dp": y * 2 + (1 - x)}, {"dp": (1 - y) * 2 + x}
    zt = [lax.rem(s + k, n) for k in range(n)]
    core = {"tensor": 1 - lax.axis_index("tensor")}
    others = [{"dp": lax.rem(d + k, 4)} for k in range(1, 4)]
    greet([{"seq": zt[k]} for k in range(1, n)] + others + [core])
    h = g_ref.shape[4] // 2
    cores = [
        send(u_ref, uo, cs.at[0], cr.at[0], core),
        send(v_ref, vo, cs.at[1], cr.at[1], core),
        send(dsmall.at[4], tsmall, cs.at[2], cr.at[2], core),
    ]
    left, right = pl.ds(0, h), pl.ds(h, h)
    single, half = jnp.float32, jnp.bfloat16
    order = list(range(1, n)) + [0]
    smalls = []
    for k in range(1, n):
        copy = send(small_ref, zsmall.at[s], s6.at[k - 1], r6.at[k - 1], {"seq": zt[k]})
        copy.start()
        smalls.append(copy)
    a1, b1, a2, b2, z1 = {}, {}, {}, {}, {}
    for j in order:
        a1[j] = send(g_ref.at[:, 1 - x, zt[j], :, left], rxa.at[j], s1.at[j], r1.at[j], xn)
        a1[j].start()
        b1[j] = send(g_ref.at[1 - y, :, zt[j], :, right], ryb.at[j], s2.at[j], r2.at[j], yn)
        b1[j].start()
    cores[0].start()
    cores[1].start()
    zsmall[s] = small_ref[...]
    for copy in smalls:
        copy.wait_recv()
    total = zsmall[0]
    for k in range(1, n):
        total = total + zsmall[k]
    dsmall[d] = total
    widely = []
    for k in range(3):
        copy = send(dsmall.at[d], dsmall.at[d], s7.at[k], r7.at[k], others[k])
        copy.start()
        widely.append(copy)

    def middle(j):
        z = zt[j]
        a1[j].wait_recv()
        ta[j] = (
            g_ref[1 - y, x, z, :, left].astype(single) + rxa[j, 1 - y].astype(single)
        ).astype(half)
        a2[j] = send(ta.at[j], rya.at[j], s3.at[j], r3.at[j], yn)
        a2[j].start()
        b1[j].wait_recv()
        tb[j] = (
            g_ref[y, 1 - x, z, :, right].astype(single) + ryb[j, 1 - x].astype(single)
        ).astype(half)
        b2[j] = send(tb.at[j], rxb.at[j], s4.at[j], r4.at[j], xn)
        b2[j].start()

    def finish(j):
        z = zt[j]
        a2[j].wait_recv()
        low = (
            g_ref[y, x, z, :, left].astype(single)
            + rxa[j, y].astype(single)
            + rya[j].astype(single)
        )
        b2[j].wait_recv()
        high = (
            g_ref[y, x, z, :, right].astype(single)
            + ryb[j, x].astype(single)
            + rxb[j].astype(single)
        )
        if j == 0:
            o_ref[:, left] = low
            o_ref[:, right] = high
        else:
            zb[j - 1, :, left] = low.astype(half)
            zb[j - 1, :, right] = high.astype(half)
            z1[j] = send(
                zb.at[j - 1], zin.at[j - 1], s5.at[j - 1], r5.at[j - 1], {"seq": zt[j]}
            )
            z1[j].start()

    for place, j in enumerate(order):
        middle(j)
        if place:
            finish(order[place - 1])
    finish(0)
    for copy in widely:
        copy.wait_recv()
    total = dsmall[0] + dsmall[1] + dsmall[2] + dsmall[3]
    dsmall[4] = total
    cores[2].start()
    for j in range(1, n):
        z1[j].wait_recv()
        o_ref[...] = o_ref[...] + zin[j - 1].astype(single)
    for copy in cores:
        copy.wait()
    edge = small_ref.shape[0] - 1
    small_o[...] = total
    small_o[edge:] = dsmall[4, edge:] + tsmall[edge:]
    for copy in smalls + widely:
        copy.wait_send()
    for group in (a1, b1, a2, b2, z1):
        for copy in group.values():
            copy.wait_send()


def reduce(grads, small, first, second, n):
    rows, columns = grads.shape[0] // (4 * n), grads.shape[1]
    h = columns // 2
    half = jnp.bfloat16
    dma = pltpu.SemaphoreType.DMA
    block = pltpu.VMEM((n, rows, h), half)
    double = pltpu.VMEM((n, 2, rows, h), half)
    row = pltpu.VMEM((n - 1, rows, columns), half)
    sems = [dma((n,))] * 8 + [dma((n - 1,))] * 4 + [dma((3,))] * 2
    return pl.pallas_call(
        functools.partial(reduce_kernel, n),
        out_shape=(
            jax.ShapeDtypeStruct((rows, columns), jnp.float32),
            jax.ShapeDtypeStruct(small.shape, jnp.float32),
            jax.ShapeDtypeStruct(first.shape, first.dtype),
            jax.ShapeDtypeStruct(second.shape, second.dtype),
        ),
        in_specs=[VMEM] * 4,
        out_specs=(VMEM,) * 4,
        scratch_shapes=[double, block, double, block, block, block, row, row]
        + [
            pltpu.VMEM((n,) + small.shape, jnp.float32),
            pltpu.VMEM((5,) + small.shape, jnp.float32),
            pltpu.VMEM(small.shape, jnp.float32),
            dma((3,)),
            dma((3,)),
        ]
        + sems,
        compiler_params=params_of(9),
    )(grads.reshape(2, 2, n, rows, columns), small, first, second)


def swish_parts(value):
    sigmoid = jax.nn.sigmoid(value)
    return (value * sigmoid, sigmoid * (1.0 + value * (1.0 - sigmoid)))


def conv_apply(padded, taps):
    tap_count = taps.shape[0] - 1
    length = padded.shape[1] - tap_count + 1
    wide = padded.astype(jnp.float32)
    total = taps[tap_count] + taps[0] * wide[:, 0:length]
    for index in range(1, tap_count):
        total = total + taps[index] * wide[:, index : index + length]
    return total


def conv_back(padded, taps, grad_pre):
    tap_count = taps.shape[0] - 1
    length = grad_pre.shape[1]
    wide = padded.astype(jnp.float32)
    tap_rows = [
        jnp.sum(grad_pre * wide[:, index : index + length], axis=(0, 1))
        for index in range(tap_count)
    ]
    tap_rows.append(jnp.sum(grad_pre, axis=(0, 1)))
    grad_pad = jnp.zeros(padded.shape, jnp.float32)
    for index in range(tap_count):
        grad_pad = grad_pad + jnp.pad(
            taps[index] * grad_pre, ((0, 0), (index, tap_count - 1 - index), (0, 0))
        )
    return (jnp.stack(tap_rows), grad_pad)


def adamw(param, moments, grad):
    first = first_decay * moments[0] + (1.0 - first_decay) * grad
    second = second_decay * moments[1] + (1.0 - second_decay) * grad * grad
    first_hat = first / (1.0 - first_decay**STEP)
    second_hat = second / (1.0 - second_decay**STEP)
    fresh = param - learn_rate * (
        first_hat / (jnp.sqrt(second_hat) + adam_epsilon) + weight_decay * param
    )
    return (fresh, jnp.stack([first, second]))


def shards(
    hidden,
    cotangent,
    gating,
    values,
    selector,
    timestep,
    output,
    prenorm,
    postnorm,
    filters,
    kernels,
    scalars,
    gating_adam,
    values_adam,
    selector_adam,
    timestep_adam,
    output_adam,
    prenorm_adam,
    postnorm_adam,
    filters_adam,
    kernels_adam,
    scalars_adam,
):
    half = jnp.bfloat16
    single = jnp.float32
    n_dp, n_seq = lax.axis_size("dp"), lax.axis_size("seq")
    core = lax.axis_index("tensor")
    seqs_dev, length, width = hidden.shape
    rows = seqs_dev * length
    own_rows = gating.shape[0]
    lead = filters.shape[0] - 2
    heads_here = timestep.shape[1]
    inner_here = gating.shape[1]
    select_here = selector.shape[1]
    conv_end = 2 * inner_here + select_here
    step_wide = 128
    in_wide = conv_end + step_wide
    packed = jnp.concatenate(
        [
            gating.astype(half),
            values.astype(half),
            selector.astype(half),
            timestep.astype(half),
            prenorm.astype(half)[:, None],
            jnp.zeros((own_rows, step_wide - heads_here - 1), half),
            output.T.astype(half),
        ],
        axis=1,
    )
    if n_dp == 4:
        weights = gather(packed, n_seq)
    else:
        weights = lax.all_gather(packed, ("dp", "seq"), axis=0, tiled=True)
    in_weight = weights[:, :in_wide]
    out_weight = weights[:, in_wide:]
    bias = scalars[0]
    rate = -jnp.exp(scalars[1])
    skip = scalars[2]
    entry_gain = weights[:, conv_end + heads_here].astype(single)
    residual = hidden.astype(single)
    entry_scale = lax.rsqrt(jnp.mean(residual * residual, axis=-1, keepdims=True) + epsilon)
    normed = (residual * entry_scale * entry_gain).astype(half)
    flat = normed.reshape(rows, width)
    raw = jnp.dot(flat, in_weight, preferred_element_type=single)
    gate_raw = raw[:, :inner_here].astype(half).reshape(seqs_dev, length, inner_here)
    conv_raw = raw[:, inner_here:conv_end].astype(half).reshape(seqs_dev, length, -1)
    delta_raw = raw[:, conv_end : conv_end + heads_here].reshape(seqs_dev, length, heads_here)
    tails = from_behind(conv_raw[:, length - lead :], "seq", 1)
    conv_pad = jnp.concatenate([tails, conv_raw], axis=1)
    taps = jnp.concatenate([filters, kernels], axis=1)
    conv_value, conv_slope = swish_parts(conv_apply(conv_pad, taps))
    conv_act = conv_value.astype(half)
    inner_act = conv_act[:, :, :inner_here]
    mine = conv_act[:, :, inner_here:]
    theirs = swap(mine.reshape(rows, select_here), 1).reshape(mine.shape)
    write_vec = jnp.where(core == 0, mine, theirs)
    read_vec = jnp.where(core == 0, theirs, mine)
    delta = jax.nn.softplus(delta_raw + bias)
    running = jnp.cumsum(delta * rate, axis=1)
    inner_h = inner_act.reshape(seqs_dev, length, heads_here, HEADDIM)
    inner_f = inner_h.astype(single)
    weight_end = jnp.exp(running[:, -1:, :] - running) * delta
    carry_decay = jnp.exp(running[:, -1, :])
    growth = jnp.exp(running)
    inner_w = (inner_f * weight_end[..., None]).astype(half)
    local_state = jnp.einsum("bthp,btn->bhpn", inner_w, write_vec, preferred_element_type=single)
    entering = carry(carry_decay, local_state, n_seq, 1, 7)
    scores = jnp.einsum("btn,bun->btu", read_vec, write_vec, preferred_element_type=single)
    causal = jnp.arange(length)[:, None] >= jnp.arange(length)[None, :]
    by_head = jnp.transpose(running, (0, 2, 1))
    gap = by_head[:, :, :, None] - by_head[:, :, None, :]
    decays = jnp.exp(jnp.where(causal, gap, -jnp.inf))
    step_head = jnp.transpose(delta, (0, 2, 1))
    mixing_b = (scores[:, None] * decays * step_head[:, :, None, :]).astype(half)
    within = jnp.einsum("bhtu,buhp->bthp", mixing_b, inner_h, preferred_element_type=single)
    across = jnp.einsum("btn,bhpn->bthp", read_vec, entering, preferred_element_type=single)
    mixer_out = (within + growth[..., None] * across + skip[None, None, :, None] * inner_f).reshape(
        seqs_dev, length, inner_here
    )
    gate_act, gate_slope = swish_parts(gate_raw.astype(single))
    gated = mixer_out * gate_act
    upstream = cotangent.reshape(rows, width)
    grad_mixed = jnp.dot(upstream, out_weight, preferred_element_type=single).reshape(
        seqs_dev, length, inner_here
    )
    hat_gated = grad_mixed * postnorm
    sums = jnp.stack([jnp.sum(gated * gated, axis=-1), jnp.sum(hat_gated * gated, axis=-1)])
    lanes = sums.reshape(-1, 128)
    sums = (lanes + swap(lanes, 2)).reshape(sums.shape)
    squares, dots = sums[0], sums[1]
    gate_scale = lax.rsqrt(squares / INNER + epsilon)[..., None]
    mixed_flat = (gated * gate_scale * postnorm).astype(half).reshape(rows, inner_here)
    branch = lax.dot_general(
        mixed_flat, out_weight, (((1,), (1,)), ((), ())), preferred_element_type=single
    ).astype(half)
    output_grad = lax.dot_general(
        upstream, mixed_flat, (((0,), (0,)), ((), ())), preferred_element_type=single
    )
    postnorm_grad = jnp.sum(grad_mixed * gated * gate_scale, axis=(0, 1))
    cube = gate_scale * gate_scale * gate_scale
    grad_gated = gate_scale * hat_gated - gated * cube * (dots / INNER)[..., None]
    grad_mixer = (grad_gated * gate_act).reshape(seqs_dev, length, heads_here, HEADDIM)
    grad_gate = (grad_gated * mixer_out * gate_slope).astype(half).reshape(rows, inner_here)

    scaled = (grad_mixer * growth[..., None]).astype(half)
    pushed = jnp.einsum("bthp,btn->bhpn", scaled, read_vec, preferred_element_type=single)
    end_grad = carry(carry_decay, pushed, n_seq, -1, 8)

    grad_half = grad_mixer.astype(half)
    skip_grad = jnp.sum(grad_mixer * inner_f, axis=(0, 1, 3))
    grad_inner = skip[None, None, :, None] * grad_mixer + jnp.einsum(
        "bhtu,bthp->buhp", mixing_b, grad_half, preferred_element_type=single
    )
    grad_mix = jnp.einsum("bthp,buhp->bhtu", grad_half, inner_h, preferred_element_type=single)
    spread_mix = grad_mix * decays
    kernel = spread_mix * scores[:, None]
    grad_delta = jnp.transpose(jnp.sum(kernel, axis=2), (0, 2, 1))
    weighted = kernel * step_head[:, :, None, :]
    grad_running = jnp.transpose(jnp.sum(weighted, axis=3) - jnp.sum(weighted, axis=2), (0, 2, 1))
    grad_scores = jnp.sum(spread_mix * step_head[:, :, None, :], axis=1).astype(half)
    grad_read = jnp.einsum("btu,bun->btn", grad_scores, write_vec, preferred_element_type=single)
    grad_write = jnp.einsum("btu,btn->bun", grad_scores, read_vec, preferred_element_type=single)
    grad_running = grad_running + jnp.sum(grad_mixer * across, axis=3) * growth
    grad_read = grad_read + jnp.einsum(
        "bthp,bhpn->btn", scaled, entering, preferred_element_type=single
    )

    decay_grad = jnp.sum(end_grad.astype(single) * entering.astype(single), axis=(2, 3))
    end_extra = decay_grad * carry_decay
    grad_xw = jnp.einsum("bhpn,btn->bthp", end_grad, write_vec, preferred_element_type=single)
    grad_write = grad_write + jnp.einsum(
        "bhpn,bthp->btn", end_grad, inner_w, preferred_element_type=single
    )
    grad_inner = grad_inner + grad_xw * weight_end[..., None]
    grad_weight = jnp.sum(grad_xw * inner_f, axis=3)
    grad_delta = grad_delta + grad_weight * jnp.exp(running[:, -1:, :] - running)
    spread = grad_weight * weight_end
    end_extra = end_extra + jnp.sum(spread, axis=1)
    grad_running = grad_running - spread
    grad_running = jnp.concatenate(
        [grad_running[:, :-1], grad_running[:, -1:] + end_extra[:, None]], axis=1
    )
    grad_log = jnp.flip(jnp.cumsum(jnp.flip(grad_running, 1), axis=1), 1)

    grad_delta = grad_delta + grad_log * rate
    alog_grad = jnp.sum(grad_log * delta, axis=(0, 1)) * rate
    grad_delta_pre = grad_delta * jax.nn.sigmoid(delta_raw + bias)
    bias_grad = jnp.sum(grad_delta_pre, axis=(0, 1))
    kept = jnp.where(core == 0, grad_write, grad_read)
    given = jnp.where(core == 0, grad_read, grad_write)
    grad_select = kept + swap(given.reshape(rows, select_here), 4).reshape(kept.shape)
    grad_conv = jnp.concatenate(
        [grad_inner.reshape(seqs_dev, length, inner_here), grad_select], axis=2
    )
    taps_grad, conv_pad_grad = conv_back(conv_pad, taps, grad_conv * conv_slope)
    back = from_behind(conv_pad_grad[:, :lead], "seq", -1)
    conv_raw_grad = (
        jnp.concatenate(
            [conv_pad_grad[:, lead:length], conv_pad_grad[:, length:] + back], axis=1
        )
        .astype(half)
        .reshape(rows, -1)
    )
    grad_all = jnp.concatenate(
        [
            grad_gate,
            conv_raw_grad,
            grad_delta_pre.astype(half).reshape(rows, heads_here),
            jnp.zeros((rows, step_wide - heads_here), half),
        ],
        axis=1,
    )
    grad_part = lax.dot_general(
        grad_all, in_weight, (((1,), (1,)), ((), ())), preferred_element_type=single
    ).astype(half)
    in_grad = lax.dot_general(
        flat, grad_all, (((0,), (0,)), ((), ())), preferred_element_type=single
    )
    prenorm_part = jnp.sum(
        grad_part.astype(single).reshape(seqs_dev, length, width) * residual * entry_scale,
        axis=(0, 1),
    )
    gain_column = conv_end + heads_here
    packed_grad = jnp.concatenate(
        [
            in_grad.astype(half),
            output_grad.astype(half),
        ],
        axis=1,
    )
    tap_rows = filters.shape[0]
    scalars_local = jnp.stack([bias_grad, alog_grad, skip_grad])
    loose = jnp.concatenate([taps_grad[:, inner_here:].reshape(-1), scalars_local.reshape(-1)])
    small = jnp.concatenate(
        [
            taps_grad[:, :inner_here],
            postnorm_grad[None],
            jnp.pad(loose, (0, inner_here - loose.shape[0]))[None],
            prenorm_part[None],
        ],
        axis=0,
    )
    if n_dp == 4:
        summed, small, branch_far, part_far = reduce(
            packed_grad, small, branch, grad_part, n_seq
        )
        prenorm_grad = small[-1]
    else:
        summed = lax.psum_scatter(
            packed_grad.astype(single), ("dp", "seq"), scatter_dimension=0, tiled=True
        )
        small = lax.psum(small, ("dp", "seq"))
        prenorm_grad = lax.psum(small[-1], "tensor")
        branch_far, part_far = swap(branch, 3), swap(grad_part, 5)
    own = lax.axis_index("dp") * n_seq + lax.axis_index("seq")
    prenorm_grad = lax.dynamic_slice_in_dim(prenorm_grad, own * own_rows, own_rows)
    branch = branch.astype(single) + branch_far.astype(single)
    result = residual + branch.reshape(seqs_dev, length, width)
    grad_part = grad_part.astype(single) + part_far.astype(single)
    grad_normed = grad_part.reshape(seqs_dev, length, width)
    hat = grad_normed * entry_gain
    hidden_grad = (
        cotangent.astype(single)
        + entry_scale * hat
        - residual
        * entry_scale
        * entry_scale
        * entry_scale
        * jnp.mean(hat * residual, axis=-1, keepdims=True)
    )
    loose_end = tap_rows * select_here
    grads = (
        summed[:, :inner_here],
        summed[:, inner_here : 2 * inner_here],
        summed[:, 2 * inner_here : conv_end],
        summed[:, conv_end:gain_column],
        summed[:, in_wide:].T,
        prenorm_grad,
        small[tap_rows],
        small[:tap_rows],
        small[tap_rows + 1, :loose_end].reshape(tap_rows, select_here),
        small[tap_rows + 1, loose_end : loose_end + 3 * heads_here].reshape(3, heads_here),
    )
    params = (
        gating,
        values,
        selector,
        timestep,
        output,
        prenorm,
        postnorm,
        filters,
        kernels,
        scalars,
    )
    moments = (
        gating_adam,
        values_adam,
        selector_adam,
        timestep_adam,
        output_adam,
        prenorm_adam,
        postnorm_adam,
        filters_adam,
        kernels_adam,
        scalars_adam,
    )
    updated = [adamw(param, moment, grad) for param, moment, grad in zip(params, moments, grads)]
    return (
        result,
        hidden_grad,
        grads[0],
        grads[1],
        grads[2],
        grads[3],
        grads[4],
        grads[5],
        grads[6],
        grads[7],
        grads[8],
        grads[9],
        updated[0][0],
        updated[1][0],
        updated[2][0],
        updated[3][0],
        updated[4][0],
        updated[5][0],
        updated[6][0],
        updated[7][0],
        updated[8][0],
        updated[9][0],
        updated[0][1],
        updated[1][1],
        updated[2][1],
        updated[3][1],
        updated[4][1],
        updated[5][1],
        updated[6][1],
        updated[7][1],
        updated[8][1],
        updated[9][1],
    )


def solution(mesh):
    placed = (
        P("dp", "seq", None),
        P("dp", "seq", None),
        P(("dp", "seq"), "tensor"),
        P(("dp", "seq"), "tensor"),
        P(("dp", "seq"), "tensor"),
        P(("dp", "seq"), "tensor"),
        P("tensor", ("dp", "seq")),
        P(("dp", "seq")),
        P("tensor"),
        P(None, "tensor"),
        P(None, "tensor"),
        P(None, "tensor"),
        P(None, ("dp", "seq"), "tensor"),
        P(None, ("dp", "seq"), "tensor"),
        P(None, ("dp", "seq"), "tensor"),
        P(None, ("dp", "seq"), "tensor"),
        P(None, "tensor", ("dp", "seq")),
        P(None, ("dp", "seq")),
        P(None, "tensor"),
        P(None, None, "tensor"),
        P(None, None, "tensor"),
        P(None, None, "tensor"),
    )
    return jax.shard_map(
        shards,
        mesh=mesh,
        in_specs=placed,
        out_specs=(
            P("dp", "seq", None),
            P("dp", "seq", None),
            P(("dp", "seq"), "tensor"),
            P(("dp", "seq"), "tensor"),
            P(("dp", "seq"), "tensor"),
            P(("dp", "seq"), "tensor"),
            P("tensor", ("dp", "seq")),
            P(("dp", "seq")),
            P("tensor"),
            P(None, "tensor"),
            P(None, "tensor"),
            P(None, "tensor"),
            P(("dp", "seq"), "tensor"),
            P(("dp", "seq"), "tensor"),
            P(("dp", "seq"), "tensor"),
            P(("dp", "seq"), "tensor"),
            P("tensor", ("dp", "seq")),
            P(("dp", "seq")),
            P("tensor"),
            P(None, "tensor"),
            P(None, "tensor"),
            P(None, "tensor"),
            P(None, ("dp", "seq"), "tensor"),
            P(None, ("dp", "seq"), "tensor"),
            P(None, ("dp", "seq"), "tensor"),
            P(None, ("dp", "seq"), "tensor"),
            P(None, "tensor", ("dp", "seq")),
            P(None, ("dp", "seq")),
            P(None, "tensor"),
            P(None, None, "tensor"),
            P(None, None, "tensor"),
            P(None, None, "tensor"),
        ),
        check_vma=False,
    )
```
